32 devices in a mesh: lon: 8 (over z, y), lat: 4 (over x, core).
Axes of the slice: x: 2, y: 2, z: 4, core: 2. Of those that a mesh axis runs over, the one named last changes fastest.
Arguments:
- tracers: float32 [4, 8, 64, 1024], P(None, None, 'lat', 'lon'), may hold values from -6 to 6
- courant_frac: float32 [8, 64, 1024], P(None, 'lat', 'lon'), may hold values from 0 to 1
- shifts: int32 [8, 64], P(None, 'lat'), may hold values from -384 to 383
- merid: float32 [8, 64, 1024], P(None, 'lat', 'lon'), may hold values from -0.9 to 0.9
Outputs:
- updated: float32 [4, 8, 64, 1024], P(None, None, 'lat', 'lon')
- zonal_flux: float32 [4, 8, 64, 1024], P(None, None, 'lat', 'lon')
The draws below stay inside these ranges and needn't reach their ends.
All inputs are finite; a program needn't handle non-finite values.
Results may differ from the reference program's by a relative error of at most 0.0003.
Values sent between devices are 32-bit elements; how exact they have to be, the bound alone decides.
No kernel may reach another device: no remote copies, remote signals or barrier semaphores. Data moves between devices by JAX's collectives and lax.ppermute only.
A program may use at most 64 MiB of HBM per device.

```python
import jax
import jax.numpy as jnp
from jax import lax

TRACERS = 4
LEV = 8
LON_DEV = 128
REACH = 3
NLAT = 64
NLON = 1024


def draw_shifts(key, part):
    rows = jnp.arange(NLAT, dtype=jnp.int32)
    spread = jnp.abs(2 * rows + 1 - NLAT)
    top = REACH * LON_DEV
    reach_row = 1 + (top - 1) * (spread * spread // (NLAT - 1)) // (NLAT - 1)
    reach_row = reach_row[None, :]
    raw_key = jax.random.fold_in(key, 11)
    sign_key = jax.random.fold_in(key, 23)
    raw = jax.random.randint(raw_key, (LEV, NLAT), 0, 1 << 20, dtype=jnp.int32)
    values = raw % (2 * reach_row) - reach_row
    signs = jax.random.randint(sign_key, (LEV, NLAT), 0, 2, dtype=jnp.int32)
    polar = (spread == NLAT - 1)[None, :]
    values = jnp.where(polar, jnp.where(signs == 1, -reach_row, reach_row - 1), values)
    level_ids = jnp.arange(LEV, dtype=jnp.int32)[:, None]
    row_ids = rows[None, :]
    values = jnp.where((level_ids == 0) & (row_ids == 0), -top, values)
    values = jnp.where((level_ids == 0) & (row_ids == NLAT - 1), top - 1, values)
    return values.astype(jnp.int32)


def block_levels(rng, extent, pieces, low, high):
    def one(axis_at, shards_of):
        draws = jax.random.uniform(jax.random.fold_in(jax.random.fold_in(rng, 6), axis_at), (shards_of,), jnp.float32, low / len(pieces), high / len(pieces))
        return jnp.repeat(jnp.exp(draws), extent[axis_at] // shards_of).reshape((-1,) + (1,) * (len(extent) - axis_at - 1))

    level = one(*pieces[0])
    for cut in pieces[1:]:
        level = level * one(*cut)
    return level


def bell_draw(own_key, shape, scale, bound, cuts=(), held_as=jnp.bfloat16):
    level = block_levels(own_key, shape, cuts, -0.22, 0.18) if cuts else 1.0
    values = jax.random.normal(own_key, shape, jnp.float32) * scale * level
    return jnp.minimum(jnp.maximum(values, -bound), bound).astype(held_as)


def setup_inputs(seed: int = 0) -> dict:
    streams_of = jax.random.split(jax.random.key(seed), 5)
    return {
        "tracers": bell_draw(streams_of[0], (TRACERS, LEV, NLAT, NLON), 1.0, 6.0, ((2, 4), (3, 8)), jnp.float32),
        "courant_frac": jnp.clip(1.0 * jax.random.uniform(streams_of[1], (LEV, NLAT, NLON), jnp.float32) ** block_levels(streams_of[1], (LEV, NLAT, NLON), ((1, 4), (2, 8)), -0.2, 0.2), 0.0, 1.0),
        "shifts": draw_shifts(jax.random.fold_in(streams_of[4], 71), 0),
        "merid": jnp.clip(jax.random.uniform(streams_of[3], (LEV, NLAT, NLON), jnp.float32, -0.9, 0.9) * block_levels(streams_of[3], (LEV, NLAT, NLON), ((1, 4), (2, 8)), -0.4, 0.0), -0.9, 0.9),
    }


def cell_part(values, slopes, weight):
    return values * weight + slopes * (weight * weight - weight) * 0.5


def advance(field, courant_frac, shifts, merid):
    levels, nrows, nlons = field.shape
    nblock = nlons // LON_DEV
    slopes = 0.5 * (jnp.roll(field, -1, axis=2) - jnp.roll(field, 1, axis=2))
    field_blocks = field.reshape(levels, nrows, nblock, LON_DEV)
    slope_blocks = slopes.reshape(levels, nrows, nblock, LON_DEV)
    totals = jnp.sum(field_blocks, axis=3)
    start_cell = (-1 - shifts).astype(jnp.int32)
    low_block = jnp.floor_divide(start_cell, LON_DEV).astype(jnp.int32)
    remain = (start_cell - low_block * LON_DEV).astype(jnp.int32)
    block_ids = jnp.arange(nblock, dtype=jnp.int32)[None, None, :]
    low_ids = (block_ids + low_block[:, :, None]) % nblock
    high_ids = (low_ids + 1) % nblock
    full_low = jnp.broadcast_to(low_ids[..., None], field_blocks.shape).astype(jnp.int32)
    full_high = jnp.broadcast_to(high_ids[..., None], field_blocks.shape).astype(jnp.int32)
    low_q = jnp.take_along_axis(field_blocks, full_low, axis=2)
    high_q = jnp.take_along_axis(field_blocks, full_high, axis=2)
    low_s = jnp.take_along_axis(slope_blocks, full_low, axis=2)
    high_s = jnp.take_along_axis(slope_blocks, full_high, axis=2)
    selector = low_block[:, :, None]
    offset_sum = jnp.zeros_like(totals)
    running = jnp.zeros_like(totals)
    for distance in range(1, REACH + 1):
        running = running + jnp.roll(totals, distance, axis=2)
        offset_sum = jnp.where(selector == -distance, -running, offset_sum)
    running = jnp.zeros_like(totals)
    for distance in range(REACH - 1):
        running = running + jnp.roll(totals, -distance, axis=2)
        offset_sum = jnp.where(selector == distance + 1, running, offset_sum)
    window_q = jnp.concatenate((low_q, high_q), axis=3)
    window_s = jnp.concatenate((low_s, high_s), axis=3)
    window_pre = jnp.cumsum(window_q, axis=3) - window_q
    cell_index = jnp.arange(LON_DEV, dtype=jnp.int32)
    index_west = jnp.broadcast_to(remain[:, :, None, None] + cell_index, field_blocks.shape).astype(jnp.int32)
    index_east = index_west + 1
    own_incl = jnp.cumsum(field_blocks, axis=3)
    own_excl = own_incl - field_blocks
    weight_east = (1.0 - courant_frac).reshape(levels, nrows, nblock, LON_DEV)
    weight_west = (1.0 - jnp.roll(courant_frac, 1, axis=2)).reshape(levels, nrows, nblock, LON_DEV)

    def pick(source, index):
        return jnp.take_along_axis(source, index, axis=3)

    flux_east = own_incl - (offset_sum[..., None] + pick(window_pre, index_east)) - cell_part(pick(window_q, index_east), pick(window_s, index_east), weight_east)
    flux_west = own_excl - (offset_sum[..., None] + pick(window_pre, index_west)) - cell_part(pick(window_q, index_west), pick(window_s, index_west), weight_west)
    flux_east = flux_east.reshape(levels, nrows, nlons)
    flux_west = flux_west.reshape(levels, nrows, nlons)
    row_ids = jnp.arange(nrows, dtype=jnp.int32)[None, :, None]
    padded = jnp.pad(field, ((0, 0), (1, 1), (0, 0)))
    side_y = 0.5 * (padded[:, 2:] - padded[:, :-2])
    side_y = jnp.where((row_ids == 0) | (row_ids == nrows - 1), 0.0, side_y)
    north_v = jnp.where(row_ids == nrows - 1, 0.0, merid)
    zero_row = jnp.zeros_like(field[:, :1])
    upper_q = jnp.concatenate((field[:, 1:], zero_row), axis=1)
    upper_s = jnp.concatenate((side_y[:, 1:], zero_row), axis=1)
    north_flux = jnp.where(north_v >= 0.0, north_v * field + north_v * (1.0 - north_v) * 0.5 * side_y, north_v * upper_q - north_v * (1.0 + north_v) * 0.5 * upper_s)
    south_flux = jnp.concatenate((zero_row, north_flux[:, :-1]), axis=1)
    updated = field - (flux_east - flux_west) - (north_flux - south_flux)
    return updated, flux_east


def reference(tracers, courant_frac, shifts, merid):
    def one_tracer(field):
        return advance(field, courant_frac, shifts, merid)

    updated, zonal_flux = lax.map(one_tracer, tracers)
    return updated, zonal_flux
```

```python
import functools

import jax
import jax.numpy as jnp
from jax import lax
from jax.experimental import pallas as pl
from jax.experimental.pallas import tpu as pltpu
from jax.sharding import PartitionSpec as P

GROUP = 4
LANES = 128


def part_rows(ref, part, levels):
    piece = ref[:, pl.ds(part * levels, levels)]
    return piece.reshape(-1, LANES)


def pack_kernel(levels, parts_ref, tracers_ref, courant_ref, *out_refs):
    for index, out_ref in enumerate(out_refs):
        part = parts_ref[index]
        quantities = part_rows(tracers_ref, part, levels)
        rows = quantities.shape[0]
        out_ref[:rows] = quantities
        out_ref[rows:] = courant_ref[pl.ds(part * levels, levels)].reshape(-1, LANES)


def split_dot(values, matrix):
    total = None
    rest = values
    for _ in range(3):
        piece = rest.astype(jnp.bfloat16)
        rest = rest - piece.astype(jnp.float32)
        product = jnp.dot(piece, matrix, preferred_element_type=jnp.float32)
        total = product if total is None else total + product
    return total


def zonal_kernel(
    blocks,
    levels,
    rows,
    tracer_count,
    meta_ref,
    shifts_ref,
    tracers_ref,
    courant_ref,
    *refs,
):
    messages = refs[: blocks - 1]
    outs = refs[blocks - 1 : blocks - 1 + GROUP]
    cells, prefix, fraction, whole, flux_all, edge = refs[blocks - 1 + GROUP :]
    pairs = levels * rows
    count = tracer_count * pairs
    part = meta_ref[0]
    own = meta_ref[1]

    def put(slot, quantities, courant):
        cells[pl.ds(pl.multiple_of(slot * count, count), count)] = quantities
        fraction[pl.ds(pl.multiple_of(slot * pairs, pairs), pairs)] = courant

    put(
        own,
        part_rows(tracers_ref, part, levels),
        courant_ref[pl.ds(part * levels, levels)].reshape(-1, LANES),
    )
    for index, message in enumerate(messages):
        put(meta_ref[2 + index], message[:count], message[count:])

    row_id = lax.broadcasted_iota(jnp.int32, (LANES, 2 * LANES), 0)
    col_id = lax.broadcasted_iota(jnp.int32, (LANES, 2 * LANES), 1)
    matrix = jnp.where(row_id <= col_id, 1.0, 0.0).astype(jnp.bfloat16)
    running = jnp.zeros((count, LANES), jnp.float32)
    for slot in range(blocks):
        sums = split_dot(cells[slot * count : (slot + 1) * count], matrix)
        prefix[slot * count : (slot + 1) * count] = sums[:, :LANES] + running
        running = running + sums[:, LANES:]
    whole[...] = running

    lane = lax.broadcasted_iota(jnp.int32, (blocks, LANES), 1)
    block_id = lax.broadcasted_iota(jnp.int32, (blocks, LANES), 0)

    def one_pair(pair, held):
        cell = -shifts_ref[part * levels + pair // rows, pair % rows]
        low = lax.shift_right_arithmetic(cell, 7)
        remain = lax.bitwise_and(cell, LANES - 1)
        lane_turn = lax.bitwise_and(LANES - remain, LANES - 1)
        block_turn = lax.rem(2 * blocks - low, blocks)
        carried = lane + remain >= LANES
        source = block_id + low + jnp.where(carried, 1, 0)
        laps = jnp.where(source < 0, -1.0, jnp.where(source >= blocks, 1.0, 0.0))

        def depart(values):
            turned = pltpu.roll(values, lane_turn, axis=1)
            near = pltpu.roll(turned, block_turn, axis=0)
            far = pltpu.roll(near, blocks - 1, axis=0)
            return jnp.where(carried, far, near)

        weight = 1.0 - fraction[pl.ds(pair, blocks, stride=pairs), :]
        half = (weight * weight - weight) * 0.25
        for tracer in range(tracer_count):
            row = tracer * pairs + pair
            values = cells[pl.ds(row, blocks, stride=count), :]
            incl = prefix[pl.ds(row, blocks, stride=count), :]
            lap = whole[pl.ds(row, 1), :]
            gone = depart(values)
            before = depart(incl - values)
            ahead = pltpu.roll(gone, LANES - 1, axis=1)
            ahead = jnp.where(lane == LANES - 1, pltpu.roll(ahead, blocks - 1, axis=0), ahead)
            behind = pltpu.roll(gone, 1, axis=1)
            behind = jnp.where(lane == 0, pltpu.roll(behind, 1, axis=0), behind)
            flux = incl - (before + lap * laps) - (gone * weight + (ahead - behind) * half)
            flux_all[pl.ds(pl.multiple_of(row * blocks, blocks), blocks), :] = flux
            spot = lax.bitwise_xor(row, 7)
            last = pltpu.roll(flux, lax.rem(spot + 1, LANES), axis=1)
            held = jnp.where(lane == spot, last, held)
        return held

    held = lax.fori_loop(0, pairs, one_pair, jnp.zeros((blocks, LANES), jnp.float32))
    edge[...] = pltpu.roll(held, 1, axis=0)
    for index, out in enumerate(outs):
        slot = meta_ref[1 + blocks + index]
        out[:count] = flux_all[pl.ds(slot, count, stride=blocks), :]
        out[count:] = jnp.broadcast_to(edge[pl.ds(slot, 1), :], (8, LANES))


def north_kernel(meta_ref, tracers_ref, merid_ref, first_ref, second_ref, out_ref):
    tracer_count, levels, rows, _ = tracers_ref.shape
    even = meta_ref[0] == 1
    bottom = meta_ref[1] == 1
    top = meta_ref[2] == 1

    row_id = lax.broadcasted_iota(jnp.int32, (rows + 2, LANES), 0)
    flat = (bottom & (row_id == 1)) | (top & (row_id == rows))

    def one_level(level, carry):
        def halo(which):
            a = first_ref[which, level]
            b = second_ref[which, level]
            north = jnp.where(even, a, b)
            south = jnp.where(even, b, a)
            return jnp.where(bottom, 0.0, south), jnp.where(top, 0.0, north)

        south_v, _ = halo(tracer_count)
        own_v = merid_ref[level]
        speed = jnp.concatenate((south_v[1:], own_v), axis=0)
        face = lax.broadcasted_iota(jnp.int32, (rows + 1, LANES), 0)
        speed = jnp.where(top & (face == rows), 0.0, speed)
        ahead = speed >= 0.0
        for tracer in range(tracer_count):
            south, north = halo(tracer)
            own = tracers_ref[tracer, level]
            band = jnp.concatenate((south, own, north), axis=0)
            side = jnp.where(flat, 0.0, 0.5 * (band[2:] - band[:-2]))
            lower = speed * band[1 : rows + 2] + speed * (1.0 - speed) * 0.5 * side[: rows + 1]
            upper = speed * band[2 : rows + 3] - speed * (1.0 + speed) * 0.5 * side[1 : rows + 2]
            flux = jnp.where(ahead, lower, upper)
            out_ref[tracer, level] = own - (flux[1:] - flux[:-1])
        return carry

    lax.fori_loop(0, levels, one_level, 0)


def final_kernel(levels, meta_ref, partial_ref, *refs):
    messages = refs[:GROUP]
    updated_ref, zonal_ref = refs[GROUP:]
    tracer_count, _, rows, _ = partial_ref.shape
    pairs = levels * rows
    count = tracer_count * pairs
    lane = lax.broadcasted_iota(jnp.int32, (8, LANES), 1)
    for index, message in enumerate(messages):
        part = meta_ref[index]
        edges = jnp.broadcast_to(message[pl.ds(count, 1), :], (8, LANES))
        for tracer in range(tracer_count):
            for level in range(levels):
                for tile in range(rows // 8):
                    base = tracer * pairs + level * rows + tile * 8
                    flux = message[base : base + 8]
                    first = pltpu.roll(edges, (LANES - 7 - base) % LANES, axis=1, stride=1, stride_axis=0)
                    west = jnp.where(lane == 0, first, pltpu.roll(flux, 1, axis=1))
                    at = (tracer, part * levels + level, pl.ds(tile * 8, 8))
                    zonal_ref[at] = flux
                    updated_ref[at] = partial_ref[at] - (flux - west)


def per_device(tracers, courant_frac, shifts, merid):
    tracer_count, all_levels, rows, _ = tracers.shape
    blocks = lax.axis_size("lon")
    me = lax.axis_index("lon")
    levels = all_levels // GROUP
    pairs = levels * rows
    count = tracer_count * pairs
    vmem = pl.BlockSpec(memory_space=pltpu.VMEM)
    smem = pl.BlockSpec(memory_space=pltpu.SMEM)
    f32 = jnp.float32

    lat = lax.axis_index("lat")
    lat_count = lax.axis_size("lat")
    even = (lat % 2 == 0).astype(jnp.int32)
    stacked = jnp.concatenate((tracers, merid[None]), axis=0)
    top_rows = stacked[:, :, rows - 2 :]
    bottom_rows = stacked[:, :, :2]

    distances = list(range(1, blocks))
    offsets = jnp.array(distances, jnp.int32)
    parts = ((me + offsets) % blocks) % GROUP
    outgoing = pl.pallas_call(
        functools.partial(pack_kernel, levels),
        out_shape=[jax.ShapeDtypeStruct((count + pairs, LANES), f32)] * len(distances),
        in_specs=[smem, vmem, vmem],
        out_specs=[vmem] * len(distances),
        name="pack",
    )(parts, tracers, courant_frac)
    arrived = [
        lax.ppermute(piece, "lon", [(i, (i + d) % blocks) for i in range(blocks)])
        for piece, d in zip(outgoing, distances)
    ]
    sources = (me - offsets) % blocks

    first = lax.ppermute(
        jnp.where(even == 1, top_rows, bottom_rows), "lat", [(i, i ^ 1) for i in range(lat_count)]
    )
    second = lax.ppermute(
        jnp.where(even == 1, bottom_rows, top_rows),
        "lat",
        [(i, (i + (1 if i % 2 else -1)) % lat_count) for i in range(lat_count)],
    )

    base = me // GROUP * GROUP
    part = me % GROUP
    near = jnp.bitwise_xor(part, jnp.arange(GROUP, dtype=jnp.int32))
    meta = jnp.concatenate((jnp.stack((part, me)), sources, base + near)).astype(jnp.int32)
    returned = pl.pallas_call(
        functools.partial(zonal_kernel, blocks, levels, rows, tracer_count),
        out_shape=[jax.ShapeDtypeStruct((count + 8, LANES), f32)] * GROUP,
        in_specs=[smem, smem] + [vmem] * (blocks + 1),
        out_specs=[vmem] * GROUP,
        scratch_shapes=[
            pltpu.VMEM((blocks * count, LANES), f32),
            pltpu.VMEM((blocks * count, LANES), f32),
            pltpu.VMEM((blocks * pairs, LANES), f32),
            pltpu.VMEM((count, LANES), f32),
            pltpu.VMEM((count * blocks, LANES), f32),
            pltpu.VMEM((blocks, LANES), f32),
        ],
        name="zonal",
    )(meta, shifts, tracers, courant_frac, *arrived)
    mine = [returned[0]] + [
        lax.ppermute(returned[x], "lon", [(i, i ^ x) for i in range(blocks)])
        for x in range(1, GROUP)
    ]

    partial = pl.pallas_call(
        north_kernel,
        out_shape=jax.ShapeDtypeStruct(tracers.shape, f32),
        in_specs=[smem] + [vmem] * 4,
        out_specs=vmem,
        name="north",
    )(
        jnp.stack((even, (lat == 0).astype(jnp.int32), (lat == lat_count - 1).astype(jnp.int32))),
        tracers,
        merid,
        first,
        second,
    )
    return pl.pallas_call(
        functools.partial(final_kernel, levels),
        out_shape=[jax.ShapeDtypeStruct(tracers.shape, f32)] * 2,
        in_specs=[smem] + [vmem] * (GROUP + 1),
        out_specs=[vmem, vmem],
        name="final",
    )(near, partial, *mine)


def solution(mesh):
    return jax.shard_map(
        per_device,
        mesh=mesh,
        in_specs=(
            P(None, None, "lat", "lon"),
            P(None, "lat", "lon"),
            P(None, "lat"),
            P(None, "lat", "lon"),
        ),
        out_specs=(P(None, None, "lat", "lon"), P(None, None, "lat", "lon")),
        check_vma=False,
    )
```

```python
import functools

import jax
import jax.numpy as jnp
from jax import lax
from jax.experimental import pallas as pl
from jax.experimental.pallas import tpu as pltpu
from jax.sharding import PartitionSpec as P


GROUP = 4
UNROLL = 8
CHUNK = 16
LIMIT = 12 * 1024 * 1024
LANES = 128


def pack_kernel(levels, tracers_ref, courant_ref, *refs):
    outs, arrivals = refs[:GROUP], refs[GROUP]
    tracer_count = tracers_ref.shape[0]
    me = lax.axis_index("lon")
    copies = []
    for index, out in enumerate(outs):
        span = pl.ds(lax.rem(me + index, GROUP) * levels, levels)
        copies += [
            pltpu.make_async_copy(
                tracers_ref.at[:, span], out.at[pl.ds(0, tracer_count)], arrivals.at[index, 0]
            ),
            pltpu.make_async_copy(
                courant_ref.at[span], out.at[tracer_count], arrivals.at[index, 1]
            ),
        ]
    for copy in copies:
        copy.start()
    for copy in copies:
        copy.wait()


def split_dot(values, matrix):
    total = None
    rest = values
    for _ in range(3):
        piece = rest.astype(jnp.bfloat16)
        rest = rest - piece.astype(jnp.float32)
        product = jnp.dot(piece, matrix, preferred_element_type=jnp.float32)
        total = product if total is None else total + product
    return total


def zonal_kernel(
    blocks,
    levels,
    rows,
    tracer_count,
    shifts_ref,
    own_ref,
    *refs,
):
    messages = (own_ref, *refs[: blocks - 1])
    outs = refs[blocks - 1 : blocks - 1 + GROUP]
    cells, local, sums, flux_all, edge, arrivals, departures = refs[blocks - 1 + GROUP :]
    pairs = levels * rows
    count = tracer_count * pairs
    me = lax.axis_index("lon")
    part = lax.rem(me, GROUP)

    incoming = []
    for distance, message in enumerate(messages):
        slot = lax.rem(me + (blocks - distance), blocks)
        copy = pltpu.make_async_copy(message, cells.at[:, slot], arrivals.at[distance])
        copy.start()
        incoming.append(copy)

    row_id = lax.broadcasted_iota(jnp.int32, (LANES, 2 * LANES), 0)
    col_id = lax.broadcasted_iota(jnp.int32, (LANES, 2 * LANES), 1)
    matrix = jnp.where(row_id <= col_id, 1.0, 0.0).astype(jnp.bfloat16)
    lane = lax.broadcasted_iota(jnp.int32, (blocks, LANES), 1)
    block_id = lax.broadcasted_iota(jnp.int32, (blocks, LANES), 0)
    for copy in incoming:
        copy.wait()

    for first in range(0, count, CHUNK):
        values = cells[first : first + CHUNK].reshape(CHUNK * blocks, LANES)
        both = split_dot(values, matrix)
        local[first : first + CHUNK] = both[:, :LANES].reshape(CHUNK, blocks, LANES)
        sums[first : first + CHUNK] = both[:, LANES:].reshape(CHUNK, blocks, LANES)

    def one_pair(pair, held):
        level = lax.div(pair, rows)
        cell = -shifts_ref[part * levels + level, pair - level * rows]
        low = lax.shift_right_arithmetic(cell, 7)
        remain = lax.bitwise_and(cell, LANES - 1)
        lane_turn = lax.bitwise_and(LANES - remain, LANES - 1)
        block_turn = lax.rem(2 * blocks - low, blocks)
        carried = lane + remain >= LANES
        source = block_id + low + jnp.where(carried, 1, 0)
        laps = jnp.where(source < 0, -1.0, jnp.where(source >= blocks, 1.0, 0.0))

        def depart(values):
            turned = pltpu.roll(values, lane_turn, axis=1)
            near = pltpu.roll(turned, block_turn, axis=0)
            far = pltpu.roll(near, blocks - 1, axis=0)
            return jnp.where(carried, far, near)

        weight = 1.0 - cells[count + pair]
        half = (weight * weight - weight) * 0.25
        for tracer in range(tracer_count):
            row = tracer * pairs + pair
            values = cells[row]
            block_sum = sums[row]
            upto = block_sum
            step = 1
            while step < blocks:
                upto = upto + jnp.where(block_id >= step, pltpu.roll(upto, step, axis=0), 0.0)
                step *= 2
            lap = upto[blocks - 1 :]
            incl = local[row] + (upto - block_sum)
            gone = depart(values)
            before = depart(incl - values)
            ahead = pltpu.roll(gone, LANES - 1, axis=1)
            ahead = jnp.where(lane == LANES - 1, pltpu.roll(ahead, blocks - 1, axis=0), ahead)
            behind = pltpu.roll(gone, 1, axis=1)
            behind = jnp.where(lane == 0, pltpu.roll(behind, 1, axis=0), behind)
            flux = incl - (before + lap * laps) - (gone * weight + (ahead - behind) * half)
            flux_all[row] = flux
            spot = lax.bitwise_xor(row, 7)
            last = pltpu.roll(flux, lax.rem(spot + 1, LANES), axis=1)
            held = jnp.where(lane == spot, last, held)
        return held

    def some_pairs(step, held):
        for index in range(UNROLL):
            held = one_pair(step * UNROLL + index, held)
        return held

    held = lax.fori_loop(0, pairs // UNROLL, some_pairs, jnp.zeros((blocks, LANES), jnp.float32))
    edge[...] = pltpu.roll(held, 1, axis=0)
    outgoing = []
    for index, out in enumerate(outs):
        slot = me - part + lax.bitwise_xor(part, index)
        pair = (
            pltpu.make_async_copy(
                flux_all.at[:, slot], out.at[pl.ds(0, count)], departures.at[index, 0]
            ),
            pltpu.make_async_copy(
                edge.at[pl.ds(slot, 1)], out.at[pl.ds(count, 1)], departures.at[index, 1]
            ),
        )
        for copy in pair:
            copy.start()
        outgoing.extend(pair)
    for copy in outgoing:
        copy.wait()


def north_kernel(lat_count, tracers_ref, merid_ref, first_ref, second_ref, out_ref):
    tracer_count, levels, rows, _ = tracers_ref.shape
    lat = lax.axis_index("lat")
    even = lax.rem(lat, 2) == 0
    bottom = lat == 0
    top = lat == lat_count - 1

    row_id = lax.broadcasted_iota(jnp.int32, (rows + 2, LANES), 0)
    flat = (bottom & (row_id == 1)) | (top & (row_id == rows))

    def one_level(level, carry):
        def halo(which):
            a = first_ref[which, level]
            b = second_ref[which, level]
            north = jnp.where(even, a, b)
            south = jnp.where(even, b, a)
            return jnp.where(bottom, 0.0, south), jnp.where(top, 0.0, north)

        south_v, _ = halo(tracer_count)
        own_v = merid_ref[level]
        speed = jnp.concatenate((south_v[1:], own_v), axis=0)
        face = lax.broadcasted_iota(jnp.int32, (rows + 1, LANES), 0)
        speed = jnp.where(top & (face == rows), 0.0, speed)
        ahead = speed >= 0.0
        for tracer in range(tracer_count):
            south, north = halo(tracer)
            own = tracers_ref[tracer, level]
            band = jnp.concatenate((south, own, north), axis=0)
            side = jnp.where(flat, 0.0, 0.5 * (band[2:] - band[:-2]))
            lower = speed * band[1 : rows + 2] + speed * (1.0 - speed) * 0.5 * side[: rows + 1]
            upper = speed * band[2 : rows + 3] - speed * (1.0 + speed) * 0.5 * side[1 : rows + 2]
            flux = jnp.where(ahead, lower, upper)
            out_ref[tracer, level] = own - (flux[1:] - flux[:-1])
        return carry

    lax.fori_loop(0, levels, one_level, 0)


def final_kernel(levels, partial_ref, *refs):
    messages = refs[:GROUP]
    updated_ref, zonal_ref, done, departures = refs[GROUP:]
    tracer_count, _, rows, _ = partial_ref.shape
    pairs = levels * rows
    count = tracer_count * pairs
    lane = lax.broadcasted_iota(jnp.int32, (8, LANES), 1)
    part = lax.rem(lax.axis_index("lon"), GROUP)
    outgoing = []
    for index, message in enumerate(messages):
        start = lax.bitwise_xor(part, index) * levels
        edges = jnp.broadcast_to(message[count : count + 1], (8, LANES))
        for tracer in range(tracer_count):
            for level in range(levels):
                for tile in range(rows // 8):
                    base = tracer * pairs + level * rows + tile * 8
                    flux = message[base : base + 8]
                    first = pltpu.roll(
                        edges, (LANES - 7 - base) % LANES, axis=1, stride=1, stride_axis=0
                    )
                    west = jnp.where(lane == 0, first, pltpu.roll(flux, 1, axis=1))
                    at = (tracer, level, slice(tile * 8, tile * 8 + 8))
                    before = partial_ref[tracer, start + level, tile * 8 : tile * 8 + 8]
                    done[(0, index, *at)] = before - (flux - west)
                    done[(1, index, *at)] = flux
        pair = (
            pltpu.make_async_copy(
                done.at[0, index], updated_ref.at[:, pl.ds(start, levels)], departures.at[index, 0]
            ),
            pltpu.make_async_copy(
                done.at[1, index], zonal_ref.at[:, pl.ds(start, levels)], departures.at[index, 1]
            ),
        )
        for copy in pair:
            copy.start()
        outgoing.extend(pair)
    for copy in outgoing:
        copy.wait()


def per_device(tracers, courant_frac, shifts, merid):
    tracer_count, all_levels, rows, _ = tracers.shape
    blocks = lax.axis_size("lon")
    levels = all_levels // GROUP
    pairs = levels * rows
    count = tracer_count * pairs
    vmem = pl.BlockSpec(memory_space=pltpu.VMEM)
    smem = pl.BlockSpec(memory_space=pltpu.SMEM)
    hbm = pl.BlockSpec(memory_space=pltpu.HBM)
    dma = pltpu.SemaphoreType.DMA
    f32 = jnp.float32

    lat = lax.axis_index("lat")
    lat_count = lax.axis_size("lat")
    even = (lat % 2 == 0).astype(jnp.int32)
    stacked = jnp.concatenate((tracers, merid[None]), axis=0)
    top_rows = stacked[:, :, rows - 2 :]
    bottom_rows = stacked[:, :, :2]

    outgoing = pl.pallas_call(
        functools.partial(pack_kernel, levels),
        out_shape=[jax.ShapeDtypeStruct((tracer_count + 1, levels, rows, LANES), f32)] * GROUP,
        in_specs=[hbm, hbm],
        out_specs=[vmem] * GROUP,
        scratch_shapes=[dma((GROUP, 2))],
        name="pack",
        compiler_params=pltpu.CompilerParams(vmem_limit_bytes=LIMIT),
    )(
        pltpu.with_memory_space_constraint(tracers, pltpu.HBM),
        pltpu.with_memory_space_constraint(courant_frac, pltpu.HBM),
    )
    outgoing = [piece.reshape(count + pairs, LANES) for piece in outgoing]
    arrived = []
    for d in range(1, blocks):
        arrived.append(
            lax.ppermute(outgoing[d % GROUP], "lon", [(i, (i + d) % blocks) for i in range(blocks)])
        )

    first = lax.ppermute(
        jnp.where(even == 1, top_rows, bottom_rows),
        "lat",
        [(i, i ^ 1) for i in range(lat_count)],
    )
    second = lax.ppermute(
        jnp.where(even == 1, bottom_rows, top_rows),
        "lat",
        [(i, (i + (1 if i % 2 else -1)) % lat_count) for i in range(lat_count)],
    )

    returned = pl.pallas_call(
        functools.partial(zonal_kernel, blocks, levels, rows, tracer_count),
        out_shape=[jax.ShapeDtypeStruct((count + 8, LANES), f32)] * GROUP,
        in_specs=[smem] + [vmem] * blocks,
        out_specs=[vmem] * GROUP,
        scratch_shapes=[
            pltpu.VMEM((count + pairs, blocks, LANES), f32),
            pltpu.VMEM((count, blocks, LANES), f32),
            pltpu.VMEM((count, blocks, LANES), f32),
            pltpu.VMEM((count, blocks, LANES), f32),
            pltpu.VMEM((blocks, LANES), f32),
            dma((blocks,)),
            dma((GROUP, 2)),
        ],
        name="zonal",
        compiler_params=pltpu.CompilerParams(vmem_limit_bytes=LIMIT),
    )(shifts, outgoing[0], *arrived)
    mine = [returned[0]]
    for x in range(1, GROUP):
        mine.append(lax.ppermute(returned[x], "lon", [(i, i ^ x) for i in range(blocks)]))

    partial = pl.pallas_call(
        functools.partial(north_kernel, lat_count),
        out_shape=jax.ShapeDtypeStruct(tracers.shape, f32),
        in_specs=[vmem] * 4,
        out_specs=vmem,
        name="north",
        compiler_params=pltpu.CompilerParams(vmem_limit_bytes=LIMIT),
    )(
        tracers,
        merid,
        first,
        second,
    )
    return pl.pallas_call(
        functools.partial(final_kernel, levels),
        out_shape=[jax.ShapeDtypeStruct(tracers.shape, f32)] * 2,
        in_specs=[vmem] * (GROUP + 1),
        out_specs=[hbm, hbm],
        scratch_shapes=[
            pltpu.VMEM((2, GROUP, tracer_count, levels, rows, LANES), f32),
            dma((GROUP, 2)),
        ],
        name="final",
        compiler_params=pltpu.CompilerParams(vmem_limit_bytes=LIMIT),
    )(partial, *mine)


def solution(mesh):
    return jax.shard_map(
        per_device,
        mesh=mesh,
        in_specs=(
            P(None, None, "lat", "lon"),
            P(None, "lat", "lon"),
            P(None, "lat"),
            P(None, "lat", "lon"),
        ),
        out_specs=(P(None, None, "lat", "lon"), P(None, None, "lat", "lon")),
        check_vma=False,
    )
```
